32 devices in a mesh: region: 8 (over z, core), grp: 4 (over y, x).
Axes of the slice: x: 2, y: 2, z: 4, core: 2. Of those that a mesh axis runs over, the one named last changes fastest.
Arguments:
- node_feats: bfloat16 [16384, 256], P(('region', 'grp')), may hold values from -6 to 6
- msg_weight: bfloat16 [256, 256], replicated, may hold values from -0.375 to 0.375
- out_weight: bfloat16 [256, 256], replicated, may hold values from -0.375 to 0.375
- adj_blocks: bfloat16 [768, 4096], P(('region', 'grp')), may hold values from -0.4375 to 0.4375
- block_row: int32 [768], P(('region', 'grp')), may hold values from 0 to 31, as said below
- block_col: int32 [768], P(('region', 'grp')), may hold values from 0 to 35, as said below
- live_counts: int32 [32, 4], P(('region', 'grp')), may hold values from 1 to 6, as said below
- cotangent: bfloat16 [16384, 256], P(('region', 'grp')), may hold values from -6 to 6
Outputs:
- layer_out: bfloat16 [16384, 256], P(('region', 'grp'))
- grad_nodes: bfloat16 [16384, 256], P(('region', 'grp'))
- grad_msg_weight: float32 [256, 256], replicated
- grad_out_weight: float32 [256, 256], replicated
The draws below stay inside these ranges and needn't reach their ends.
Inputs may be any that keep to these rules, and one draw needn't show every extreme that they name: `block_row`: on every device, slots o * 6 to (o + 1) * 6 - 1 hold blocks whose row block lies from o * 8 to (o + 1) * 8 - 1, the node blocks owned by member o of the device's group. `block_col`: A value c under 2 names the previous region's last 2 node blocks, a value of 34 or more the next region's first ones, any other value the region's block c - 2. Of a device's slots for owner o, the first live_counts[d, o] are in use and the rest are padding; in each region some owner receives 6 slots in use from every device of its group.
All inputs are finite; a program needn't handle non-finite values.
Results may differ from the reference program's by a relative error of at most 0.0056.
Values may be sent and summed in bfloat16 or wider, within the bound.
No kernel may reach another device: no remote copies, remote signals or barrier semaphores. Data moves between devices by JAX's collectives and lax.ppermute only.
A program may use at most 64 MiB of HBM per device.

```python
import math
import jax
import jax.numpy as jnp
from jax import lax

WIDTH = 256
BLOCK = 64
HALO_BLOCKS = 2
SLOTS_OWNER = 6
MEMBERS = 4
REGIONS = 8
NODE_BLOCKS = 8
REGION_BLOCKS = 32
SLOTS_DEV = 24
BLOCKS = 768
NODES = 16384
DEVICES = 32


def draw_block_row(key, part):
    slot_ids = jnp.arange(BLOCKS, dtype=jnp.int32)
    owner = slot_ids % SLOTS_DEV // SLOTS_OWNER
    return (owner * NODE_BLOCKS + jax.random.randint(key, (BLOCKS,), 0, NODE_BLOCKS, dtype=jnp.int32)).astype(jnp.int32)


def draw_block_col(key, part):
    row_of_slot = draw_block_row(key, part)
    first_key = jax.random.fold_in(key, 11)
    second_key = jax.random.fold_in(key, 12)
    third_key = jax.random.fold_in(key, 13)
    fourth_key = jax.random.fold_in(key, 14)
    near_rim = jax.random.randint(first_key, (BLOCKS,), 0, 8, dtype=jnp.int32) == 0
    which_side = jax.random.randint(second_key, (BLOCKS,), 0, 2, dtype=jnp.int32)
    offset = jax.random.randint(third_key, (BLOCKS,), 0, HALO_BLOCKS, dtype=jnp.int32)
    band_step = jax.random.randint(fourth_key, (BLOCKS,), -6, 7, dtype=jnp.int32)
    inner = jnp.clip(row_of_slot + HALO_BLOCKS + band_step, 0, REGION_BLOCKS + 2 * HALO_BLOCKS - 1)
    rim_col = offset + which_side * (REGION_BLOCKS + HALO_BLOCKS)
    return jnp.where(near_rim, rim_col, inner).astype(jnp.int32)


def draw_live_counts(key, part):
    first_key, second_key = jax.random.split(key, 2)
    base = jax.random.randint(first_key, (DEVICES, MEMBERS), max(1, SLOTS_OWNER // 4), SLOTS_OWNER + 1, dtype=jnp.int32)
    hottest = jax.random.randint(second_key, (REGIONS,), 0, MEMBERS, dtype=jnp.int32)
    hot_device = jnp.repeat(hottest, MEMBERS, total_repeat_length=DEVICES)
    full_row = jnp.arange(MEMBERS, dtype=jnp.int32)[None, :] == hot_device[:, None]
    return jnp.where(full_row, SLOTS_OWNER, base).astype(jnp.int32)


def block_levels(stream_key, extent, cuts, least, high):
    level = 1.0
    for dim, shards_of in cuts:
        draws = jax.random.uniform(jax.random.fold_in(jax.random.fold_in(stream_key, 6), dim), (shards_of,), jnp.float32, least / len(cuts), high / len(cuts))
        level = level * jnp.repeat(jnp.exp(draws), extent[dim] // shards_of).reshape((-1,) + (1,) * (len(extent) - 1 - dim))
    return level


def centred(rng, shape, spread, most, pieces=(), kind=jnp.bfloat16):
    drawn = jax.random.normal(rng, shape, jnp.float32) * spread
    if len(pieces) > 0:
        drawn = block_levels(rng, shape, pieces, -0.22, 0.18) * drawn
    return jnp.clip(drawn, min=-most, max=most).astype(kind)


def setup_inputs(seed: int = 0) -> dict:
    seeds = jax.random.split(jax.random.key(seed), 9)
    node_feats = centred(seeds[0], (NODES, WIDTH), 1.0, 6.0, ((0, 32),))
    msg_weight = centred(seeds[1], (WIDTH, WIDTH), WIDTH ** -0.5, 0.375)
    out_weight = centred(seeds[2], (WIDTH, WIDTH), WIDTH ** -0.5, 0.375)
    adj_blocks = centred(seeds[3], (BLOCKS, BLOCK * BLOCK), (MEMBERS * SLOTS_OWNER * BLOCK // NODE_BLOCKS) ** -0.5, 0.4375, ((0, 32),))
    block_row = draw_block_row(jax.random.fold_in(seeds[8], 71), 0)
    block_col = draw_block_col(jax.random.fold_in(seeds[8], 71), 0)
    live_counts = draw_live_counts(jax.random.fold_in(seeds[8], 71), 0)
    cotangent = centred(seeds[7], (NODES, WIDTH), 1.0, 6.0, ((0, 32),))
    return dict(node_feats=node_feats, msg_weight=msg_weight, out_weight=out_weight, adj_blocks=adj_blocks, block_row=block_row, block_col=block_col, live_counts=live_counts, cotangent=cotangent)


def reference(node_feats, msg_weight, out_weight, adj_blocks, block_row, block_col, live_counts, cotangent):
    group_size = math.gcd(SLOTS_DEV, 64)
    turn_count = BLOCKS // group_size
    all_blocks = REGIONS * REGION_BLOCKS
    slot_ids = jnp.arange(BLOCKS, dtype=jnp.int32)
    device = (slot_ids // SLOTS_DEV).astype(jnp.int32)
    position = (slot_ids % SLOTS_DEV).astype(jnp.int32)
    region = (device // MEMBERS).astype(jnp.int32)
    in_use = (position % SLOTS_OWNER) < live_counts[device, (position // SLOTS_OWNER).astype(jnp.int32)]
    global_row = (region * REGION_BLOCKS + block_row).astype(jnp.int32)
    padded_col = (region * REGION_BLOCKS + block_col).astype(jnp.int32)
    tile_group = adj_blocks.reshape(turn_count, group_size, BLOCK, BLOCK)
    row_ids = global_row.reshape(turn_count, group_size)
    col_ids = padded_col.reshape(turn_count, group_size)
    use_ids = in_use.reshape(turn_count, group_size)
    message = jnp.dot(node_feats, msg_weight, preferred_element_type=jnp.float32).astype(jnp.bfloat16)
    zero_rim = jnp.zeros((HALO_BLOCKS * BLOCK, WIDTH), jnp.bfloat16)
    source = jnp.concatenate([zero_rim, message, zero_rim], axis=0).reshape(all_blocks + 2 * HALO_BLOCKS, BLOCK, WIDTH)

    def forward(running, scan_entry):
        tiles_now, rows_now, cols_now, use_now = scan_entry
        gathered = source[cols_now].astype(jnp.float32)
        product = jnp.einsum("kij,kjw->kiw", tiles_now.astype(jnp.float32), gathered)
        product = jnp.where(use_now[:, None, None], product, 0.0)
        return running.at[rows_now].add(product), None

    aggregate, _ = lax.scan(forward, jnp.zeros((all_blocks, BLOCK, WIDTH), jnp.float32), (tile_group, row_ids, col_ids, use_ids))
    aggregate = aggregate.reshape(NODES, WIDTH)
    hidden = jax.nn.silu(aggregate).astype(jnp.bfloat16)
    layer_out = (node_feats.astype(jnp.float32) + jnp.dot(hidden, out_weight, preferred_element_type=jnp.float32)).astype(jnp.bfloat16)
    sigmoid_val = jax.nn.sigmoid(aggregate)
    upstream = jnp.dot(cotangent, out_weight.T, preferred_element_type=jnp.float32)
    grad_pre = (upstream * sigmoid_val * (1.0 + aggregate * (1.0 - sigmoid_val))).astype(jnp.bfloat16)
    grad_blocks = grad_pre.reshape(all_blocks, BLOCK, WIDTH)

    def backward(running, scan_entry):
        tiles_now, rows_now, cols_now, use_now = scan_entry
        gathered = grad_blocks[rows_now].astype(jnp.float32)
        product = jnp.einsum("kji,kjw->kiw", tiles_now.astype(jnp.float32), gathered)
        product = jnp.where(use_now[:, None, None], product, 0.0)
        return running.at[cols_now].add(product), None

    returned, _ = lax.scan(backward, jnp.zeros((all_blocks + 2 * HALO_BLOCKS, BLOCK, WIDTH), jnp.float32), (tile_group, row_ids, col_ids, use_ids))
    grad_msg = returned[HALO_BLOCKS:HALO_BLOCKS + all_blocks].reshape(NODES, WIDTH).astype(jnp.bfloat16)
    grad_nodes = (cotangent.astype(jnp.float32) + jnp.dot(grad_msg, msg_weight.T, preferred_element_type=jnp.float32)).astype(jnp.bfloat16)
    grad_msg_weight = jnp.dot(node_feats.T, grad_msg, preferred_element_type=jnp.float32)
    grad_out_weight = jnp.dot(hidden.T, cotangent, preferred_element_type=jnp.float32)
    return layer_out, grad_nodes, grad_msg_weight, grad_out_weight
```

```python
import functools

import jax
import jax.numpy as jnp
from jax import lax
from jax.experimental import pallas as pl
from jax.experimental.pallas import tpu as pltpu
from jax.sharding import PartitionSpec as P

BLOCK = 64
HALO_BLOCKS = 2
QUAD = 4
BF16 = jnp.bfloat16
F32 = jnp.float32
VMEM = pl.BlockSpec(memory_space=pltpu.VMEM)
SMEM = pl.BlockSpec(memory_space=pltpu.SMEM)
LIMIT = 24 << 20


def dot(a, b, ca=1, cb=0):
    return lax.dot_general(a, b, (((ca,), (cb,)), ((), ())), preferred_element_type=F32)


def slot_masks(width):
    lane = lax.broadcasted_iota(jnp.int32, (BLOCK, width), 1) // BLOCK
    return [jnp.where(lane == j, 1.0, 0.0).astype(BF16) for j in range(QUAD)]


def for_each_quad(adj_refs, idx_ref, quads, body):
    masks = slot_masks(QUAD * BLOCK)
    slots = len(adj_refs) * quads * QUAD
    for p, adj in enumerate(adj_refs):

        def step(q, carry, adj=adj, p=p):
            tile = adj[pl.ds(pl.multiple_of(q * BLOCK, BLOCK), BLOCK), :]
            diagonal = jnp.concatenate([tile * m for m in masks], axis=0)
            first = (p * quads + q) * QUAD
            rows = [pl.multiple_of(idx_ref[first + j], BLOCK) for j in range(QUAD)]
            cols = [pl.multiple_of(idx_ref[slots + first + j], BLOCK) for j in range(QUAD)]
            body(diagonal, rows, cols)
            return carry

        lax.fori_loop(0, quads, step, 0, unroll=quads <= 8)


def forward_kernel(members, quads, idx_ref, *refs):
    nf, refs = refs[:members], refs[members:]
    prev, nxt, refs = refs[0], refs[1], refs[2:]
    adj, refs = refs[:members], refs[members:]
    wm, wo, rowsum, hidden, slope, layer_out, source, acc = refs
    n = nf[0].shape[0]
    h = prev.shape[0]
    total = members * n
    for p in range(members):
        source[p * n : (p + 1) * n, :] = nf[p][...]
    source[total : total + h, :] = prev[...]
    source[total + h : total + 2 * h, :] = nxt[...]
    acc[...] = jnp.zeros_like(acc)

    def add(diagonal, rows, cols):
        taken = jnp.concatenate([source[pl.ds(c, BLOCK), :] for c in cols], axis=0)
        out = dot(diagonal, taken)
        for j, r in enumerate(rows):
            acc[pl.ds(r, BLOCK), :] += out[j * BLOCK : (j + 1) * BLOCK]

    for_each_quad(adj, idx_ref, quads, add)
    chunk = 256

    def finish(i, carry):
        at = pl.ds(pl.multiple_of(i * chunk, chunk), chunk)
        b = acc[at, :].astype(BF16)
        rowsum[at, :] = b
        agg = dot(b, wm[...])
        s = 1.0 / (1.0 + jnp.exp(-agg))
        hidden[at, :] = (agg * s).astype(BF16)
        slope[at, :] = s * (1.0 + agg * (1.0 - s))
        return carry

    lax.fori_loop(0, total // chunk, finish, 0)
    layer_out[...] = (nf[0][...].astype(F32) + dot(hidden[:n, :], wo[...])).astype(BF16)


def upstream_kernel(members, split, me_ref, *refs):
    cot, refs = refs[:members], refs[members:]
    rowsum, hidden, slope, wo, grad_pre, part = refs
    n = cot[0].shape[0]
    for p in range(members):
        up = dot(cot[p][...], wo[...], 1, 1)
        grad_pre[p * n : (p + 1) * n, :] = (up * slope[p * n : (p + 1) * n, :]).astype(BF16)
    width = rowsum.shape[1]
    if split:
        deep = part.shape[0]
        half = members // 2
        me = me_ref[0]
        lanes = pl.ds(pl.multiple_of(lax.rem(me, half) * deep, deep), deep)

        @pl.when(me < half)
        def _():
            part[...] = dot(rowsum[:, lanes], grad_pre[...], 0, 0)

        @pl.when(me >= half)
        def _():
            total = dot(hidden[:n, lanes], cot[0][...], 0, 0)
            for p in range(1, members):
                total += dot(hidden[p * n : (p + 1) * n, lanes], cot[p][...], 0, 0)
            part[...] = total
    else:
        part[:width, :] = dot(rowsum[...], grad_pre[...], 0, 0)
        total = dot(hidden[:n, :], cot[0][...], 0, 0)
        for p in range(1, members):
            total += dot(hidden[p * n : (p + 1) * n, :], cot[p][...], 0, 0)
        part[width:, :] = total


def backward_kernel(members, quads, idx_ref, me_ref, *refs):
    adj, refs = refs[:members], refs[members:]
    grad_pre, own, rim, acc = refs
    total = grad_pre.shape[0]
    h = rim.shape[0]
    acc[...] = jnp.zeros_like(acc)

    def add(diagonal, rows, cols):
        taken = jnp.concatenate([grad_pre[pl.ds(r, BLOCK), :] for r in rows], axis=0)
        out = dot(diagonal, taken, 0, 0)
        for j, c in enumerate(cols):
            acc[pl.ds(c, BLOCK), :] += out[j * BLOCK : (j + 1) * BLOCK]

    for_each_quad(adj, idx_ref, quads, add)
    own[...] = acc[: own.shape[0], :]
    first = jnp.where(me_ref[0] == 0, total, total + h)
    rim[...] = acc[pl.ds(pl.multiple_of(first, h), h), :]


def nodes_kernel(members, me_ref, own, arrived, cot, wm, out):
    n = own.shape[0]
    h = arrived.shape[0]
    me = me_ref[0]
    head = jnp.where(me == 0, arrived[...], 0.0)
    tail = jnp.where(me == members - 1, arrived[...], 0.0)
    zeros = jnp.zeros((n - 2 * h, own.shape[1]), F32)
    grad_msg = (own[...] + jnp.concatenate([head, zeros, tail], axis=0)).astype(BF16)
    out[...] = (cot[...].astype(F32) + dot(grad_msg, wm[...], 1, 1)).astype(BF16)


def call(kernel, outs, in_specs, scratch, flops, args, limit=LIMIT):
    moved = sum(a.size * a.dtype.itemsize for a in (*args, *outs))
    return pl.pallas_call(
        kernel,
        out_shape=outs,
        in_specs=in_specs,
        out_specs=[VMEM] * len(outs),
        scratch_shapes=scratch,
        compiler_params=pltpu.CompilerParams(vmem_limit_bytes=limit),
        cost_estimate=pl.CostEstimate(flops=flops, bytes_accessed=moved, transcendentals=0),
    )(*args)


def partners(members):
    return [[(i, i ^ k) for i in range(members)] for k in range(1, members)]


def gather(value):
    members = lax.axis_size("grp")
    return [value] + [lax.ppermute(value, "grp", perm) for perm in partners(members)]


def tree_sum(values):
    while len(values) > 1:
        values = [values[i] + values[i + 1] for i in range(0, len(values), 2)]
    return values[0]


def per_device(
    node_feats, msg_weight, out_weight, adj_blocks, block_row, block_col, live_counts, cotangent
):
    n, width = node_feats.shape
    members = lax.axis_size("grp")
    regions = lax.axis_size("region")
    me = lax.axis_index("grp")
    node_blocks = n // BLOCK
    region_blocks = members * node_blocks
    slots = adj_blocks.shape[0]
    quads = slots // QUAD
    per_owner = slots // members
    halo = HALO_BLOCKS * BLOCK
    total = members * n
    limit = LIMIT if members <= 4 else 60 << 20

    nf = gather(node_feats)

    slot_ids = jnp.arange(slots, dtype=jnp.int32)
    in_use = slot_ids % per_owner < jnp.repeat(
        live_counts[0], per_owner, total_repeat_length=slots
    )
    kept = jnp.where(in_use[:, None], adj_blocks, jnp.zeros((), BF16))
    tiles = kept.reshape(quads, QUAD, BLOCK, BLOCK).transpose(0, 2, 1, 3)
    tiles = tiles.reshape(quads * BLOCK, QUAD * BLOCK)
    ids = jnp.stack([block_row, block_col]).astype(BF16)
    ids = jnp.pad(ids, ((0, 14), (0, QUAD * BLOCK - slots)))
    adj = gather(jnp.concatenate([tiles, ids], axis=0))

    cot = gather(cotangent)

    ids = jnp.stack([a[quads * BLOCK : quads * BLOCK + 2, :slots] for a in adj], axis=1)
    ids = ids.astype(jnp.int32).reshape(2, members * slots)
    rows, cols = ids[0], ids[1] - HALO_BLOCKS

    def place(block):
        return ((block // node_blocks) ^ me) * node_blocks + block % node_blocks

    outside = jnp.where(cols < 0, region_blocks + HALO_BLOCKS + cols, HALO_BLOCKS + cols)
    inside = (cols >= 0) & (cols < region_blocks)
    idx = jnp.concatenate([place(rows), jnp.where(inside, place(cols), outside)]) * BLOCK
    me_arr = me.reshape(1).astype(jnp.int32)

    first, last = nf[0], nf[0]
    for k in range(1, members):
        first = jnp.where(me ^ k == 0, nf[k], first)
        last = jnp.where(me ^ k == members - 1, nf[k], last)
    up = [(i, i + 1) for i in range(regions - 1)]
    down = [(i + 1, i) for i in range(regions - 1)]
    prev = lax.ppermute(last[n - halo :], "region", up)
    nxt = lax.ppermute(first[:halo], "region", down)

    sds = jax.ShapeDtypeStruct
    rowsum, hidden, slope, layer_out = call(
        functools.partial(forward_kernel, members, quads),
        [
            sds((total, width), BF16),
            sds((total, width), BF16),
            sds((total, width), F32),
            sds((n, width), BF16),
        ],
        [SMEM] + [VMEM] * (2 * members + 4),
        [pltpu.VMEM((total + 2 * halo, width), BF16), pltpu.VMEM((total, width), F32)],
        2 * members * quads * 256**3,
        (idx, *nf, prev, nxt, *adj, msg_weight, out_weight),
        limit,
    )
    deep = 2 * width // members
    split = deep % 128 == 0
    grad_pre, part = call(
        functools.partial(upstream_kernel, members, split),
        [sds((total, width), BF16), sds((deep if split else 2 * width, width), F32)],
        [SMEM] + [VMEM] * (members + 4),
        [],
        4 * total * width * width,
        (me_arr, *cot, rowsum, hidden, slope, out_weight),
        limit,
    )
    if not split:
        part = lax.dynamic_slice_in_dim(part, me * deep, deep, 0)

    def swap(value, k):
        return lax.ppermute(value, "region", [(i, i ^ k) for i in range(regions)])

    def rounded(value):
        return lax.reduce_precision(value, 8, 7).astype(BF16)

    pair = rounded(part + swap(part, 1))
    layers = [pair] + [swap(pair, 2 * k) for k in range(1, regions // 2)]
    reduced = rounded(tree_sum([v.astype(F32) for v in layers]))
    pieces = gather(reduced)
    stacked = jnp.zeros((2 * width, width), F32)
    for k, piece in enumerate(pieces):
        stacked = lax.dynamic_update_slice(stacked, piece.astype(F32), ((me ^ k) * deep, 0))

    own, rim = call(
        functools.partial(backward_kernel, members, quads),
        [sds((n, width), F32), sds((halo, width), F32)],
        [SMEM, SMEM] + [VMEM] * (members + 1),
        [pltpu.VMEM((total + 2 * halo, width), F32)],
        2 * members * quads * 256**3,
        (idx, me_arr, *adj, grad_pre),
        limit,
    )
    across = []
    for r in range(regions - 1):
        across.append((r * members + members - 1, (r + 1) * members))
        across.append(((r + 1) * members, r * members + members - 1))
    arrived = lax.ppermute(rim, ("region", "grp"), across)
    (grad_nodes,) = call(
        functools.partial(nodes_kernel, members),
        [sds((n, width), BF16)],
        [SMEM] + [VMEM] * 4,
        [],
        2 * n * width * width,
        (me_arr, own, arrived, cotangent, msg_weight),
    )
    return (layer_out, grad_nodes, stacked[:width], stacked[width:])


def solution(mesh):
    in_specs = (
        P(("region", "grp"), None),
        P(),
        P(),
        P(("region", "grp"), None),
        P(("region", "grp")),
        P(("region", "grp")),
        P(("region", "grp"), None),
        P(("region", "grp"), None),
    )
    out_specs = (P(("region", "grp"), None), P(("region", "grp"), None), P(), P())
    return jax.shard_map(
        per_device, mesh=mesh, in_specs=in_specs, out_specs=out_specs, check_vma=False
    )
```

```python
import functools

import jax
import jax.numpy as jnp
from jax import lax
from jax.experimental import pallas as pl
from jax.experimental.pallas import tpu as pltpu
from jax.sharding import PartitionSpec as P

BLOCK = 64
HALO_BLOCKS = 2
QUAD = 4
ID_ROWS = 16
ID_LANES = 128
BF16 = jnp.bfloat16
F32 = jnp.float32
VMEM = pl.BlockSpec(memory_space=pltpu.VMEM)
SMEM = pl.BlockSpec(memory_space=pltpu.SMEM)


def dot(a, b, ca=1, cb=0):
    return lax.dot_general(a, b, (((ca,), (cb,)), ((), ())), preferred_element_type=F32)


def aligned(value, unit):
    return value if isinstance(value, int) else pl.multiple_of(value, unit)


class Shape:
    def __init__(self, n, width, slots, members, regions):
        self.n, self.width, self.slots = n, width, slots
        self.members, self.regions = members, regions
        self.quads = slots // QUAD
        self.per_owner = slots // members
        self.halo = HALO_BLOCKS * BLOCK
        self.total = members * n
        self.ext = self.total + 2 * self.halo
        self.tiles = self.quads * BLOCK


def for_each_quad(shape, me, ids, tiles, body):
    lane = lax.broadcasted_iota(jnp.int32, (BLOCK, QUAD * BLOCK), 1) // BLOCK
    masks = [jnp.where(lane == j, 1.0, 0.0).astype(BF16) for j in range(QUAD)]

    def step(p, q):
        first = aligned((p * shape.quads + q) * BLOCK, BLOCK)
        tile = tiles[pl.ds(first, BLOCK), :]
        diagonal = jnp.concatenate([tile * m for m in masks], axis=0)
        place = (p ^ me) * 3
        rows, cols, used = [], [], []
        for j in range(QUAD):
            slot = q * QUAD + j
            rows.append(pl.multiple_of(ids[place, slot] * BLOCK, BLOCK))
            cols.append(pl.multiple_of(ids[place + 1, slot] * BLOCK, BLOCK))
            if isinstance(slot, int):
                owner, nth = divmod(slot, shape.per_owner)
            else:
                owner, nth = lax.div(slot, shape.per_owner), lax.rem(slot, shape.per_owner)
            used.append(nth < ids[place + 2, owner])
        body(diagonal, rows, cols, used)

    if shape.members * shape.quads <= 32:
        for p in range(shape.members):
            for q in range(shape.quads):
                step(p, q)
    else:

        def flat(i, carry):
            step(lax.div(i, shape.quads), lax.rem(i, shape.quads))
            return carry

        lax.fori_loop(0, shape.members * shape.quads, flat, 0)


def put(me, layout, refs, into, size, first=0):
    for (k, start, rows), ref in zip(layout, refs):
        rows = min(rows, size - start)
        at = pl.multiple_of((me ^ k) * size + start + first, 8)
        into[pl.ds(at, rows), :] = ref[:rows, :]


def forward_kernel(shape, nf_layout, adj_layout, where, ids, *refs):
    nf, refs = refs[: len(nf_layout)], refs[len(nf_layout) :]
    adj, refs = refs[: len(adj_layout)], refs[len(adj_layout) :]
    prev, nxt, wm, wo, rowsum, hidden, slope, layer_out, tiles, source, acc = refs
    me = where[0]
    h, n, total = shape.halo, shape.n, shape.total
    source[:h, :] = prev[...]
    put(me, nf_layout, nf, source, n, h)
    source[h + total :, :] = nxt[...]
    put(me, adj_layout, adj, tiles, shape.tiles)
    acc[...] = jnp.zeros_like(acc)

    def add(diagonal, rows, cols, used):
        taken = jnp.concatenate([source[pl.ds(c, BLOCK), :] for c in cols], axis=0)
        out = dot(diagonal, taken)
        for j in range(QUAD):
            at = pl.ds(pl.multiple_of(jnp.where(used[j], rows[j], total), BLOCK), BLOCK)
            acc[at, :] += out[j * BLOCK : (j + 1) * BLOCK]

    for_each_quad(shape, me, ids, tiles, add)
    chunk = 256

    def finish(i, carry):
        at = pl.ds(pl.multiple_of(i * chunk, chunk), chunk)
        b = acc[at, :].astype(BF16)
        rowsum[at, :] = b
        agg = dot(b, wm[...])
        s = 1.0 / (1.0 + jnp.exp(-agg))
        hidden[at, :] = (agg * s).astype(BF16)
        slope[at, :] = s * (1.0 + agg * (1.0 - s))
        return carry

    lax.fori_loop(0, total // chunk, finish, 0)
    own = pl.ds(pl.multiple_of(me * n, n), n)
    layer_out[...] = (nf[0][...].astype(F32) + dot(hidden[own, :], wo[...])).astype(BF16)


def upstream_kernel(shape, layout, where, *refs):
    cot, refs = refs[: len(layout)], refs[len(layout) :]
    rowsum, hidden, slope, wo, grad_pre, keep, give, whole = refs
    me, core = where[0], where[1]
    put(me, layout, cot, whole, shape.n)
    chunk = min(shape.n, 512)
    for i in range(0, shape.total, chunk):
        up = dot(whole[i : i + chunk, :], wo[...], 1, 1)
        grad_pre[i : i + chunk, :] = (up * slope[i : i + chunk, :]).astype(BF16)
    half = shape.width // 2
    mine = pl.ds(pl.multiple_of(core * half, half), half)
    other = pl.ds(pl.multiple_of((1 - core) * half, half), half)

    @pl.when(me % 2 == 0)
    def _():
        give[...] = dot(rowsum[:, other], grad_pre[...], 0, 0)
        keep[...] = dot(rowsum[:, mine], grad_pre[...], 0, 0)

    @pl.when(me % 2 == 1)
    def _():
        give[...] = dot(hidden[:, other], whole[...], 0, 0)
        keep[...] = dot(hidden[:, mine], whole[...], 0, 0)


def backward_kernel(shape, where, ids, tiles, grad_pre, own, rim, acc):
    me = where[0]
    h, n = shape.halo, shape.n
    acc[...] = jnp.zeros_like(acc)

    def add(diagonal, rows, cols, used):
        taken = jnp.concatenate([grad_pre[pl.ds(r, BLOCK), :] for r in rows], axis=0)
        out = dot(diagonal, taken, 0, 0)
        for j in range(QUAD):
            at = pl.ds(pl.multiple_of(jnp.where(used[j], cols[j], shape.ext), BLOCK), BLOCK)
            acc[at, :] += out[j * BLOCK : (j + 1) * BLOCK]

    for_each_quad(shape, me, ids, tiles, add)
    own[...] = acc[pl.ds(pl.multiple_of(h + me * n, BLOCK), n), :]
    first = jnp.where(me == 0, 0, h + shape.total)
    rim[...] = acc[pl.ds(pl.multiple_of(first, h), h), :]


def nodes_kernel(shape, where, own, arrived, cot, wm, out):
    me = where[0]
    head = jnp.where(me == 0, arrived[...], 0.0)
    tail = jnp.where(me == shape.members - 1, arrived[...], 0.0)
    zeros = jnp.zeros((shape.n - 2 * shape.halo, shape.width), F32)
    grad_msg = (own[...] + jnp.concatenate([head, zeros, tail], axis=0)).astype(BF16)
    out[...] = (cot[...].astype(F32) + dot(grad_msg, wm[...], 1, 1)).astype(BF16)


def weights_kernel(where, own, across, beside, both, msg, out):
    me, core = where[0], where[1]
    half = own.shape[0]
    mine = pl.ds(pl.multiple_of(core * half, half), half)
    other = pl.ds(pl.multiple_of((1 - core) * half, half), half)

    @pl.when(me % 2 == 0)
    def _():
        msg[mine, :] = own[...].astype(F32)
        msg[other, :] = across[...].astype(F32)
        out[mine, :] = beside[...].astype(F32)
        out[other, :] = both[...].astype(F32)

    @pl.when(me % 2 == 1)
    def _():
        out[mine, :] = own[...].astype(F32)
        out[other, :] = across[...].astype(F32)
        msg[mine, :] = beside[...].astype(F32)
        msg[other, :] = both[...].astype(F32)


def call(kernel, outs, scalars, args, scratch, flops, limit):
    moved = sum(a.size * a.dtype.itemsize for a in (*args, *outs))
    return pl.pallas_call(
        kernel,
        out_shape=outs,
        in_specs=[SMEM] * len(scalars) + [VMEM] * len(args),
        out_specs=[VMEM] * len(outs),
        scratch_shapes=scratch,
        compiler_params=pltpu.CompilerParams(vmem_limit_bytes=limit),
        cost_estimate=pl.CostEstimate(flops=flops, bytes_accessed=moved, transcendentals=0),
    )(*scalars, *args)


def swap(value, axis, k):
    return lax.ppermute(value, axis, [(i, i ^ k) for i in range(lax.axis_size(axis))])


def gather(value):
    members = lax.axis_size("grp")
    rows = value.shape[0]
    if members != 4:
        pieces = [value] + [swap(value, "grp", k) for k in range(1, members)]
        return pieces, tuple((k, 0, rows) for k in range(members))
    half = rows // 2
    x, y = swap(value, "grp", 1), swap(value, "grp", 2)
    low, high = swap(x[:half], "grp", 2), swap(y[half:], "grp", 1)
    layout = ((0, 0, rows), (1, 0, rows), (2, 0, rows), (3, 0, half), (3, half, rows - half))
    return [value, x, y, low, high], layout


def tree_sum(values):
    while len(values) > 1:
        values = [values[i] + values[i + 1] for i in range(0, len(values), 2)]
    return values[0]


def rounded(value):
    return lax.reduce_precision(value, 8, 7).astype(BF16)


def per_device(
    node_feats, msg_weight, out_weight, adj_blocks, block_row, block_col, live_counts, cotangent
):
    n, width = node_feats.shape
    slots = adj_blocks.shape[0]
    members, regions = lax.axis_size("grp"), lax.axis_size("region")
    shape = Shape(n, width, slots, members, regions)
    h, total = shape.halo, shape.total
    me, region = lax.axis_index("grp"), lax.axis_index("region")
    where = jnp.stack([me, region % 2]).astype(jnp.int32)
    limit = (20 << 20) if members <= 4 else (60 << 20)

    nf, nf_layout = gather(node_feats)

    tiles = adj_blocks.reshape(shape.quads, QUAD, BLOCK, BLOCK).transpose(0, 2, 1, 3)
    tiles = tiles.reshape(shape.tiles, QUAD * BLOCK)
    lanes = QUAD * BLOCK
    live = live_counts[0]
    ids = jnp.stack(
        [jnp.pad(v.astype(BF16), (0, lanes - v.shape[0])) for v in (block_row, block_col, live)]
    )
    ids = jnp.pad(ids, ((0, ID_ROWS - 3), (0, 0)))
    adj, adj_layout = gather(jnp.concatenate([tiles, ids], axis=0))

    cot, cot_layout = gather(cotangent)

    found = [
        a[shape.tiles - start : shape.tiles - start + 3, :ID_LANES]
        for (_, start, rows), a in zip(adj_layout, adj)
        if start + rows > shape.tiles
    ]
    ids = jnp.concatenate(found, axis=0).astype(jnp.int32)

    firsts, lasts = {}, {}
    for (k, start, rows), piece in zip(nf_layout, nf):
        if start == 0:
            firsts[k] = piece[:h]
        if start + rows == n:
            lasts[k] = piece[rows - h :]
    first, last = firsts[0], lasts[0]
    for k in range(1, members):
        first = jnp.where(me == k, firsts[k], first)
        last = jnp.where(me ^ k == members - 1, lasts[k], last)
    prev = lax.ppermute(last, "region", [(i, i + 1) for i in range(regions - 1)])
    nxt = lax.ppermute(first, "region", [(i + 1, i) for i in range(regions - 1)])

    sds = jax.ShapeDtypeStruct
    half = width // 2
    spmm_flops = 2 * members * shape.quads * 256**3
    rowsum, hidden, slope, layer_out, tiles = call(
        functools.partial(forward_kernel, shape, nf_layout, adj_layout),
        [
            sds((total, width), BF16),
            sds((total, width), BF16),
            sds((total, width), F32),
            sds((n, width), BF16),
            sds((members * shape.tiles, QUAD * BLOCK), BF16),
        ],
        (where, ids),
        (*nf, *adj, prev, nxt, msg_weight, out_weight),
        [pltpu.VMEM((shape.ext, width), BF16), pltpu.VMEM((total + BLOCK, width), F32)],
        spmm_flops,
        limit,
    )
    grad_pre, keep, give = call(
        functools.partial(upstream_kernel, shape, cot_layout),
        [sds((total, width), BF16), sds((half, width), F32), sds((half, width), F32)],
        (where,),
        (*cot, rowsum, hidden, slope, out_weight),
        [pltpu.VMEM((total, width), BF16)],
        4 * total * width * width,
        limit,
    )
    pair = rounded(keep + swap(give, "region", 1))
    layers = [pair] + [swap(pair, "region", 2 * k) for k in range(1, regions // 2)]
    reduced = rounded(tree_sum([v.astype(F32) for v in layers]))
    across = swap(reduced, "region", 1)
    beside = swap(reduced, "grp", 1)
    both = swap(beside, "region", 1)

    own, rim = call(
        functools.partial(backward_kernel, shape),
        [sds((n, width), F32), sds((h, width), F32)],
        (where, ids),
        (tiles, grad_pre),
        [pltpu.VMEM((shape.ext + BLOCK, width), F32)],
        spmm_flops,
        limit,
    )
    pairs = []
    for r in range(regions - 1):
        pairs.append((r * members + members - 1, (r + 1) * members))
        pairs.append(((r + 1) * members, r * members + members - 1))
    arrived = lax.ppermute(rim, ("region", "grp"), pairs)
    (grad_nodes,) = call(
        functools.partial(nodes_kernel, shape),
        [sds((n, width), BF16)],
        (where,),
        (own, arrived, cotangent, msg_weight),
        [],
        2 * n * width * width,
        limit,
    )
    grad_msg_weight, grad_out_weight = call(
        weights_kernel,
        [sds((width, width), F32), sds((width, width), F32)],
        (where,),
        (reduced, across, beside, both),
        [],
        0,
        limit,
    )
    return (layer_out, grad_nodes, grad_msg_weight, grad_out_weight)


def solution(mesh):
    in_specs = (
        P(("region", "grp"), None),
        P(),
        P(),
        P(("region", "grp"), None),
        P(("region", "grp")),
        P(("region", "grp")),
        P(("region", "grp"), None),
        P(("region", "grp"), None),
    )
    out_specs = (P(("region", "grp"), None), P(("region", "grp"), None), P(), P())
    return jax.shard_map(
        per_device, mesh=mesh, in_specs=in_specs, out_specs=out_specs, check_vma=False
    )
```

```python
import functools

import jax
import jax.numpy as jnp
from jax import lax
from jax.experimental import pallas as pl
from jax.experimental.pallas import tpu as pltpu
from jax.sharding import PartitionSpec as P

BLOCK = 64
HALO_BLOCKS = 2
QUAD = 4
ID_ROWS = 16
BF16 = jnp.bfloat16
F32 = jnp.float32
VMEM = pl.BlockSpec(memory_space=pltpu.VMEM)
SMEM = pl.BlockSpec(memory_space=pltpu.SMEM)


def dot(a, b, ca=1, cb=0):
    return lax.dot_general(a, b, (((ca,), (cb,)), ((), ())), preferred_element_type=F32)


def aligned(value, unit):
    return value if isinstance(value, int) else pl.multiple_of(value, unit)


class Shape:
    def __init__(self, n, width, slots, members, regions):
        self.n, self.width, self.slots = n, width, slots
        self.members, self.regions = members, regions
        self.quads = slots // QUAD
        self.per_owner = slots // members
        self.halo = HALO_BLOCKS * BLOCK
        self.total = members * n
        self.ext = self.total + 2 * self.halo
        self.tiles = self.quads * BLOCK


def for_each_quad(shape, me, ids, tiles, body):
    lane = lax.broadcasted_iota(jnp.int32, (BLOCK, QUAD * BLOCK), 1) // BLOCK
    masks = [jnp.where(lane == j, 1.0, 0.0).astype(BF16) for j in range(QUAD)]

    def step(p, q):
        first = aligned((p * shape.quads + q) * BLOCK, BLOCK)
        tile = tiles[pl.ds(first, BLOCK), :]
        diagonal = jnp.concatenate([tile * m for m in masks], axis=0)
        place = p ^ me
        rows, cols, used = [], [], []
        for j in range(QUAD):
            slot = q * QUAD + j
            rows.append(pl.multiple_of(ids[place, slot] * BLOCK, BLOCK))
            cols.append(pl.multiple_of(ids[place, shape.slots + slot] * BLOCK, BLOCK))
            if isinstance(slot, int):
                owner, nth = divmod(slot, shape.per_owner)
            else:
                owner, nth = lax.div(slot, shape.per_owner), lax.rem(slot, shape.per_owner)
            used.append(nth < ids[place, 2 * shape.slots + owner])
        body(diagonal, rows, cols, used)

    if shape.members * shape.quads <= 32:
        for p in range(shape.members):
            for q in range(shape.quads):
                step(p, q)
    else:

        def flat(i, carry):
            step(lax.div(i, shape.quads), lax.rem(i, shape.quads))
            return carry

        lax.fori_loop(0, shape.members * shape.quads, flat, 0)


def put(me, layout, refs, into, size, first=0):
    for (k, start, rows), ref in zip(layout, refs):
        rows = min(rows, size - start)
        at = pl.multiple_of((me ^ k) * size + start + first, 8)
        into[pl.ds(at, rows), :] = ref[:rows, :]


def forward_kernel(shape, nf_layout, adj_layout, where, ids, *refs):
    nf, refs = refs[: len(nf_layout)], refs[len(nf_layout) :]
    adj, refs = refs[: len(adj_layout)], refs[len(adj_layout) :]
    prev, nxt, wm, wo, rowsum, hidden, slope, layer_out, tiles, source, acc = refs
    me = where[0]
    h, n, total = shape.halo, shape.n, shape.total
    source[:h, :] = prev[...]
    put(me, nf_layout, nf, source, n, h)
    source[h + total :, :] = nxt[...]
    put(me, adj_layout, adj, tiles, shape.tiles)
    acc[...] = jnp.zeros_like(acc)

    def add(diagonal, rows, cols, used):
        taken = jnp.concatenate([source[pl.ds(c, BLOCK), :] for c in cols], axis=0)
        out = dot(diagonal, taken)
        for j in range(QUAD):
            at = pl.ds(pl.multiple_of(jnp.where(used[j], rows[j], total), BLOCK), BLOCK)
            acc[at, :] += out[j * BLOCK : (j + 1) * BLOCK]

    for_each_quad(shape, me, ids, tiles, add)
    chunk = 256

    def finish(i, carry):
        at = pl.ds(pl.multiple_of(i * chunk, chunk), chunk)
        b = acc[at, :].astype(BF16)
        rowsum[at, :] = b
        agg = dot(b, wm[...])
        s = 0.5 * jnp.tanh(0.5 * agg) + 0.5
        hidden[at, :] = (agg * s).astype(BF16)
        slope[at, :] = s * (1.0 + agg * (1.0 - s))
        return carry

    lax.fori_loop(0, total // chunk, finish, 0, unroll=total // chunk <= 8)
    own = pl.ds(pl.multiple_of(me * n, n), n)
    layer_out[...] = (nf[0][...].astype(F32) + dot(hidden[own, :], wo[...])).astype(BF16)


def upstream_kernel(shape, layout, where, *refs):
    cot, refs = refs[: len(layout)], refs[len(layout) :]
    rowsum, hidden, slope, wo, grad_pre, keep, give, whole = refs
    me, core = where[0], where[1]
    put(me, layout, cot, whole, shape.n)
    chunk = min(shape.n, 512)
    for i in range(0, shape.total, chunk):
        up = dot(whole[i : i + chunk, :], wo[...], 1, 1)
        grad_pre[i : i + chunk, :] = (up * slope[i : i + chunk, :]).astype(BF16)
    half = shape.width // 2
    mine = pl.ds(pl.multiple_of(core * half, half), half)
    other = pl.ds(pl.multiple_of((1 - core) * half, half), half)

    @pl.when(me % 2 == 0)
    def _():
        give[...] = dot(rowsum[:, other], grad_pre[...], 0, 0)
        keep[...] = dot(rowsum[:, mine], grad_pre[...], 0, 0)

    @pl.when(me % 2 == 1)
    def _():
        give[...] = dot(hidden[:, other], whole[...], 0, 0)
        keep[...] = dot(hidden[:, mine], whole[...], 0, 0)


def backward_kernel(shape, where, ids, tiles, grad_pre, own, rim, acc):
    me = where[0]
    h, n = shape.halo, shape.n
    acc[...] = jnp.zeros_like(acc)

    def add(diagonal, rows, cols, used):
        taken = jnp.concatenate([grad_pre[pl.ds(r, BLOCK), :] for r in rows], axis=0)
        out = dot(diagonal, taken, 0, 0)
        for j in range(QUAD):
            at = pl.ds(pl.multiple_of(jnp.where(used[j], cols[j], shape.ext), BLOCK), BLOCK)
            acc[at, :] += out[j * BLOCK : (j + 1) * BLOCK]

    for_each_quad(shape, me, ids, tiles, add)
    own[...] = acc[pl.ds(pl.multiple_of(h + me * n, BLOCK), n), :]
    first = jnp.where(me == 0, 0, h + shape.total)
    rim[...] = acc[pl.ds(pl.multiple_of(first, h), h), :].astype(BF16)


def nodes_kernel(shape, where, own, arrived, cot, wm, out):
    me = where[0]
    rim = arrived[...].astype(F32)
    head = jnp.where(me == 0, rim, 0.0)
    tail = jnp.where(me == shape.members - 1, rim, 0.0)
    zeros = jnp.zeros((shape.n - 2 * shape.halo, shape.width), F32)
    grad_msg = (own[...] + jnp.concatenate([head, zeros, tail], axis=0)).astype(BF16)
    out[...] = (cot[...].astype(F32) + dot(grad_msg, wm[...], 1, 1)).astype(BF16)


def weights_kernel(where, own, across, beside, both, msg, out):
    me, core = where[0], where[1]
    half = own.shape[0]
    mine = pl.ds(pl.multiple_of(core * half, half), half)
    other = pl.ds(pl.multiple_of((1 - core) * half, half), half)

    @pl.when(me % 2 == 0)
    def _():
        msg[mine, :] = own[...].astype(F32)
        msg[other, :] = across[...].astype(F32)
        out[mine, :] = beside[...].astype(F32)
        out[other, :] = both[...].astype(F32)

    @pl.when(me % 2 == 1)
    def _():
        out[mine, :] = own[...].astype(F32)
        out[other, :] = across[...].astype(F32)
        msg[mine, :] = beside[...].astype(F32)
        msg[other, :] = both[...].astype(F32)


def call(kernel, outs, scalars, args, scratch, flops, limit):
    moved = sum(a.size * a.dtype.itemsize for a in (*args, *outs))
    return pl.pallas_call(
        kernel,
        out_shape=outs,
        in_specs=[SMEM] * len(scalars) + [VMEM] * len(args),
        out_specs=[VMEM] * len(outs),
        scratch_shapes=scratch,
        compiler_params=pltpu.CompilerParams(vmem_limit_bytes=limit),
        cost_estimate=pl.CostEstimate(flops=flops, bytes_accessed=moved, transcendentals=0),
    )(*scalars, *args)


def swap(value, axis, k):
    return lax.ppermute(value, axis, [(i, i ^ k) for i in range(lax.axis_size(axis))])


def gather(value, after=()):
    members = lax.axis_size("grp")
    rows = value.shape[0]
    if members != 4:
        pieces = [value] + [swap(value, "grp", k) for k in range(1, members)]
        return pieces, tuple((k, 0, rows) for k in range(members))
    half = rows // 2
    x, y = swap(value, "grp", 1), swap(value, "grp", 2)
    low, high, _ = lax.optimization_barrier((x[:half], y[half:], after))
    low, high = swap(low, "grp", 2), swap(high, "grp", 1)
    layout = ((0, 0, rows), (1, 0, rows), (2, 0, rows), (3, 0, half), (3, half, rows - half))
    return [value, x, y, low, high], layout


def tree_sum(values):
    while len(values) > 1:
        values = [values[i] + values[i + 1] for i in range(0, len(values), 2)]
    return values[0]


def rounded(value):
    return lax.reduce_precision(value, 8, 7).astype(BF16)


def per_device(
    node_feats, msg_weight, out_weight, adj_blocks, block_row, block_col, live_counts, cotangent
):
    n, width = node_feats.shape
    slots = adj_blocks.shape[0]
    members, regions = lax.axis_size("grp"), lax.axis_size("region")
    shape = Shape(n, width, slots, members, regions)
    h, total = shape.halo, shape.total
    me, region = lax.axis_index("grp"), lax.axis_index("region")
    where = jnp.stack([me, region % 2]).astype(jnp.int32)
    limit = (20 << 20) if members <= 4 else (60 << 20)

    nf, nf_layout = gather(node_feats)

    tiles = adj_blocks.reshape(shape.quads, QUAD, BLOCK, BLOCK).transpose(0, 2, 1, 3)
    tiles = tiles.reshape(shape.tiles, QUAD * BLOCK)
    lanes = QUAD * BLOCK
    ids = jnp.concatenate([block_row, block_col, live_counts[0]]).astype(BF16)[None]
    ids = jnp.pad(ids, ((0, ID_ROWS - 1), (0, lanes - ids.shape[1])))
    adj, adj_layout = gather(jnp.concatenate([tiles, ids], axis=0))

    found = [
        a[shape.tiles - start : shape.tiles - start + 1]
        for (_, start, rows), a in zip(adj_layout, adj)
        if start + rows > shape.tiles
    ]
    ids = jnp.concatenate(found, axis=0).astype(jnp.int32)

    firsts, lasts = {}, {}
    for (k, start, rows), piece in zip(nf_layout, nf):
        if start == 0:
            firsts[k] = piece[:h]
        if start + rows == n:
            lasts[k] = piece[rows - h :]
    first, last = firsts[0], lasts[0]
    for k in range(1, members):
        first = jnp.where(me == k, firsts[k], first)
        last = jnp.where(me ^ k == members - 1, lasts[k], last)
    late = lax.optimization_barrier((cotangent, nf[1:3]))[0]
    cot, cot_layout = gather(late, (first, last))

    prev = lax.ppermute(last, "region", [(i, i + 1) for i in range(regions - 1)])
    nxt = lax.ppermute(first, "region", [(i + 1, i) for i in range(regions - 1)])

    sds = jax.ShapeDtypeStruct
    half = width // 2
    unit = members * shape.quads * 2 * 256**3
    rowsum, hidden, slope, layer_out, tiles = call(
        functools.partial(forward_kernel, shape, nf_layout, adj_layout),
        [
            sds((total, width), BF16),
            sds((total, width), BF16),
            sds((total, width), F32),
            sds((n, width), BF16),
            sds((members * shape.tiles, QUAD * BLOCK), BF16),
        ],
        (where, ids),
        (*nf, *adj, prev, nxt, msg_weight, out_weight),
        [pltpu.VMEM((shape.ext, width), BF16), pltpu.VMEM((total + BLOCK, width), F32)],
        7 * unit,
        limit,
    )
    grad_pre, keep, give = call(
        functools.partial(upstream_kernel, shape, cot_layout),
        [sds((total, width), BF16), sds((half, width), F32), sds((half, width), F32)],
        (where,),
        (*cot, rowsum, hidden, slope, out_weight),
        [pltpu.VMEM((total, width), BF16)],
        2 * unit,
        limit,
    )
    pair = rounded(keep + swap(give, "region", 1))
    layers = [pair] + [swap(pair, "region", 2 * k) for k in range(1, regions // 2)]
    reduced = rounded(tree_sum([v.astype(F32) for v in layers]))
    across = swap(reduced, "region", 1)
    beside = swap(reduced, "grp", 1)
    diagonal = [
        (r * members + m, (r ^ 1) * members + (m ^ 1))
        for r in range(regions)
        for m in range(members)
    ]
    both = lax.ppermute(reduced, ("region", "grp"), diagonal)
    own, rim = call(
        functools.partial(backward_kernel, shape),
        [sds((n, width), F32), sds((h, width), BF16)],
        (where, ids),
        (tiles, grad_pre),
        [pltpu.VMEM((shape.ext + BLOCK, width), F32)],
        3 * unit,
        limit,
    )
    pairs = []
    for r in range(regions - 1):
        pairs.append((r * members + members - 1, (r + 1) * members))
        pairs.append(((r + 1) * members, r * members + members - 1))
    arrived = lax.ppermute(rim, ("region", "grp"), pairs)
    (grad_nodes,) = call(
        functools.partial(nodes_kernel, shape),
        [sds((n, width), BF16)],
        (where,),
        (own, arrived, cotangent, msg_weight),
        [],
        2 * unit,
        limit,
    )
    grad_msg_weight, grad_out_weight = call(
        weights_kernel,
        [sds((width, width), F32), sds((width, width), F32)],
        (where,),
        (reduced, across, beside, both),
        [],
        0,
        limit,
    )
    return (layer_out, grad_nodes, grad_msg_weight, grad_out_weight)


def solution(mesh):
    in_specs = (
        P(("region", "grp"), None),
        P(),
        P(),
        P(("region", "grp"), None),
        P(("region", "grp")),
        P(("region", "grp")),
        P(("region", "grp"), None),
        P(("region", "grp"), None),
    )
    out_specs = (P(("region", "grp"), None), P(("region", "grp"), None), P(), P())
    return jax.shard_map(
        per_device, mesh=mesh, in_specs=in_specs, out_specs=out_specs, check_vma=False
    )
```

```python
import functools

import jax
import jax.numpy as jnp
from jax import lax
from jax.experimental import pallas as pl
from jax.experimental.pallas import tpu as pltpu
from jax.sharding import PartitionSpec as P

BLOCK = 64
HALO_BLOCKS = 2
QUAD = 4
ID_ROWS = 16
BF16 = jnp.bfloat16
F32 = jnp.float32
VMEM = pl.BlockSpec(memory_space=pltpu.VMEM)
SMEM = pl.BlockSpec(memory_space=pltpu.SMEM)


def dot(a, b, ca=1, cb=0):
    return lax.dot_general(a, b, (((ca,), (cb,)), ((), ())), preferred_element_type=F32)


def aligned(value, unit):
    return value if isinstance(value, int) else pl.multiple_of(value, unit)


class Shape:
    def __init__(self, n, width, slots, members, regions):
        self.n, self.width, self.slots = n, width, slots
        self.members, self.regions = members, regions
        self.quads = slots // QUAD
        self.per_owner = slots // members
        self.halo = HALO_BLOCKS * BLOCK
        self.total = members * n
        self.ext = self.total + 2 * self.halo
        self.tiles = self.quads * BLOCK


def for_each_quad(shape, me, ids, tiles, body):
    lane = lax.broadcasted_iota(jnp.int32, (BLOCK, QUAD * BLOCK), 1) // BLOCK
    masks = [jnp.where(lane == j, 1.0, 0.0).astype(BF16) for j in range(QUAD)]

    def step(p, q):
        first = aligned((p * shape.quads + q) * BLOCK, BLOCK)
        tile = tiles[pl.ds(first, BLOCK), :]
        diagonal = jnp.concatenate([tile * m for m in masks], axis=0)
        place = p ^ me
        rows, cols, used = [], [], []
        for j in range(QUAD):
            slot = q * QUAD + j
            rows.append(pl.multiple_of(ids[place, slot] * BLOCK, BLOCK))
            cols.append(pl.multiple_of(ids[place, shape.slots + slot] * BLOCK, BLOCK))
            if isinstance(slot, int):
                owner, nth = divmod(slot, shape.per_owner)
            else:
                owner, nth = lax.div(slot, shape.per_owner), lax.rem(slot, shape.per_owner)
            used.append(nth < ids[place, 2 * shape.slots + owner])
        body(diagonal, rows, cols, used)

    if shape.members * shape.quads <= 32:
        for p in range(shape.members):
            for q in range(shape.quads):
                step(p, q)
    else:

        def flat(i, carry):
            step(lax.div(i, shape.quads), lax.rem(i, shape.quads))
            return carry

        lax.fori_loop(0, shape.members * shape.quads, flat, 0)


def put(me, layout, refs, into, size, first=0):
    for (k, start, rows), ref in zip(layout, refs):
        rows = min(rows, size - start)
        at = pl.multiple_of((me ^ k) * size + start + first, 8)
        into[pl.ds(at, rows), :] = ref[:rows, :]


def forward_kernel(shape, nf_layout, adj_layout, where, ids, *refs):
    nf, refs = refs[: len(nf_layout)], refs[len(nf_layout) :]
    adj, refs = refs[: len(adj_layout)], refs[len(adj_layout) :]
    prev, nxt, wm, wo, rowsum, hidden, slope, layer_out, tiles, source, acc = refs
    me = where[0]
    h, n, total = shape.halo, shape.n, shape.total
    source[:h, :] = prev[...]
    put(me, nf_layout, nf, source, n, h)
    source[h + total :, :] = nxt[...]
    put(me, adj_layout, adj, tiles, shape.tiles)
    acc[...] = jnp.zeros_like(acc)

    def add(diagonal, rows, cols, used):
        taken = jnp.concatenate([source[pl.ds(c, BLOCK), :] for c in cols], axis=0)
        out = dot(diagonal, taken)
        for j in range(QUAD):
            at = pl.ds(pl.multiple_of(jnp.where(used[j], rows[j], total), BLOCK), BLOCK)
            acc[at, :] += out[j * BLOCK : (j + 1) * BLOCK]

    for_each_quad(shape, me, ids, tiles, add)
    chunk = 256

    def finish(i, carry):
        at = pl.ds(pl.multiple_of(i * chunk, chunk), chunk)
        b = acc[at, :].astype(BF16)
        rowsum[at, :] = b
        agg = dot(b, wm[...])
        s = 0.5 * jnp.tanh(0.5 * agg) + 0.5
        hidden[at, :] = (agg * s).astype(BF16)
        slope[at, :] = s * (1.0 + agg * (1.0 - s))
        return carry

    lax.fori_loop(0, total // chunk, finish, 0, unroll=total // chunk <= 8)
    own = pl.ds(pl.multiple_of(me * n, n), n)
    layer_out[...] = (nf[0][...].astype(F32) + dot(hidden[own, :], wo[...])).astype(BF16)


def upstream_kernel(shape, layout, where, *refs):
    cot, refs = refs[: len(layout)], refs[len(layout) :]
    rowsum, hidden, slope, wo, grad_pre, keep, give, whole = refs
    me, core = where[0], where[1]
    put(me, layout, cot, whole, shape.n)
    chunk = min(shape.n, 512)
    for i in range(0, shape.total, chunk):
        up = dot(whole[i : i + chunk, :], wo[...], 1, 1)
        grad_pre[i : i + chunk, :] = (up * slope[i : i + chunk, :]).astype(BF16)
    half = shape.width // 2
    mine = pl.ds(pl.multiple_of(core * half, half), half)
    other = pl.ds(pl.multiple_of((1 - core) * half, half), half)

    @pl.when(me % 2 == 0)
    def _():
        give[...] = dot(rowsum[:, other], grad_pre[...], 0, 0)
        keep[...] = dot(rowsum[:, mine], grad_pre[...], 0, 0)

    @pl.when(me % 2 == 1)
    def _():
        give[...] = dot(hidden[:, other], whole[...], 0, 0)
        keep[...] = dot(hidden[:, mine], whole[...], 0, 0)


def backward_kernel(shape, where, ids, tiles, grad_pre, own, rim, acc):
    me = where[0]
    h, n = shape.halo, shape.n
    acc[...] = jnp.zeros_like(acc)

    def add(diagonal, rows, cols, used):
        taken = jnp.concatenate([grad_pre[pl.ds(r, BLOCK), :] for r in rows], axis=0)
        out = dot(diagonal, taken, 0, 0)
        for j in range(QUAD):
            at = pl.ds(pl.multiple_of(jnp.where(used[j], cols[j], shape.ext), BLOCK), BLOCK)
            acc[at, :] += out[j * BLOCK : (j + 1) * BLOCK]

    for_each_quad(shape, me, ids, tiles, add)
    own[...] = acc[pl.ds(pl.multiple_of(h + me * n, BLOCK), n), :]
    first = jnp.where(me == 0, 0, h + shape.total)
    rim[...] = acc[pl.ds(pl.multiple_of(first, h), h), :].astype(BF16)


def nodes_kernel(shape, where, own, arrived, cot, wm, out):
    me = where[0]
    rim = arrived[...].astype(F32)
    head = jnp.where(me == 0, rim, 0.0)
    tail = jnp.where(me == shape.members - 1, rim, 0.0)
    zeros = jnp.zeros((shape.n - 2 * shape.halo, shape.width), F32)
    grad_msg = (own[...] + jnp.concatenate([head, zeros, tail], axis=0)).astype(BF16)
    out[...] = (cot[...].astype(F32) + dot(grad_msg, wm[...], 1, 1)).astype(BF16)


def weights_kernel(where, own, across, beside, both, msg, out):
    me, core = where[0], where[1]
    half = own.shape[0]
    mine = pl.ds(pl.multiple_of(core * half, half), half)
    other = pl.ds(pl.multiple_of((1 - core) * half, half), half)

    @pl.when(me % 2 == 0)
    def _():
        msg[mine, :] = own[...].astype(F32)
        msg[other, :] = across[...].astype(F32)
        out[mine, :] = beside[...].astype(F32)
        out[other, :] = both[...].astype(F32)

    @pl.when(me % 2 == 1)
    def _():
        out[mine, :] = own[...].astype(F32)
        out[other, :] = across[...].astype(F32)
        msg[mine, :] = beside[...].astype(F32)
        msg[other, :] = both[...].astype(F32)


def call(kernel, outs, scalars, args, scratch, flops, limit):
    moved = sum(a.size * a.dtype.itemsize for a in (*args, *outs))
    return pl.pallas_call(
        kernel,
        out_shape=outs,
        in_specs=[SMEM] * len(scalars) + [VMEM] * len(args),
        out_specs=[VMEM] * len(outs),
        scratch_shapes=scratch,
        compiler_params=pltpu.CompilerParams(vmem_limit_bytes=limit),
        cost_estimate=pl.CostEstimate(flops=flops, bytes_accessed=moved, transcendentals=0),
    )(*scalars, *args)


def swap(value, axis, k):
    return lax.ppermute(value, axis, [(i, i ^ k) for i in range(lax.axis_size(axis))])


def gather(value, after=()):
    members = lax.axis_size("grp")
    rows = value.shape[0]
    if members != 4:
        pieces = [value] + [swap(value, "grp", k) for k in range(1, members)]
        return pieces, tuple((k, 0, rows) for k in range(members))
    half = rows // 2
    x, y = swap(value, "grp", 1), swap(value, "grp", 2)
    low, high, _ = lax.optimization_barrier((x[:half], y[half:], after))
    low, high = swap(low, "grp", 2), swap(high, "grp", 1)
    layout = ((0, 0, rows), (1, 0, rows), (2, 0, rows), (3, 0, half), (3, half, rows - half))
    return [value, x, y, low, high], layout


def tree_sum(values):
    while len(values) > 1:
        values = [values[i] + values[i + 1] for i in range(0, len(values), 2)]
    return values[0]


def rounded(value):
    return lax.reduce_precision(value, 8, 7).astype(BF16)


def per_device(
    node_feats, msg_weight, out_weight, adj_blocks, block_row, block_col, live_counts, cotangent
):
    n, width = node_feats.shape
    slots = adj_blocks.shape[0]
    members, regions = lax.axis_size("grp"), lax.axis_size("region")
    shape = Shape(n, width, slots, members, regions)
    h, total = shape.halo, shape.total
    me, region = lax.axis_index("grp"), lax.axis_index("region")
    where = jnp.stack([me, region % 2]).astype(jnp.int32)
    limit = (20 << 20) if members <= 4 else (60 << 20)

    nf, nf_layout = gather(node_feats)

    tiles = adj_blocks.reshape(shape.quads, QUAD, BLOCK, BLOCK).transpose(0, 2, 1, 3)
    tiles = tiles.reshape(shape.tiles, QUAD * BLOCK)
    lanes = QUAD * BLOCK
    ids = jnp.concatenate([block_row, block_col, live_counts[0]]).astype(BF16)[None]
    ids = jnp.pad(ids, ((0, ID_ROWS - 1), (0, lanes - ids.shape[1])))
    adj, adj_layout = gather(jnp.concatenate([tiles, ids], axis=0))

    firsts, lasts = {}, {}
    for (k, start, rows), piece in zip(nf_layout, nf):
        if start == 0:
            firsts[k] = piece[:h]
        if start + rows == n:
            lasts[k] = piece[rows - h :]
    first, last = firsts[0], lasts[0]
    for k in range(1, members):
        first = jnp.where(me == k, firsts[k], first)
        last = jnp.where(me ^ k == members - 1, lasts[k], last)
    late = lax.optimization_barrier((cotangent, nf[3:]))[0]
    cot, cot_layout = gather(late)

    prev = lax.ppermute(last, "region", [(i, i + 1) for i in range(regions - 1)])
    nxt = lax.ppermute(first, "region", [(i + 1, i) for i in range(regions - 1)])

    held = adj[:3] + lax.optimization_barrier((adj[3:], prev, nxt))[0]
    found = [
        a[shape.tiles - start : shape.tiles - start + 1]
        for (_, start, rows), a in zip(adj_layout, held)
        if start + rows > shape.tiles
    ]
    ids = jnp.concatenate(found, axis=0).astype(jnp.int32)

    sds = jax.ShapeDtypeStruct
    half = width // 2
    unit = members * shape.quads * 2 * 256**3
    rowsum, hidden, slope, layer_out, tiles = call(
        functools.partial(forward_kernel, shape, nf_layout, adj_layout),
        [
            sds((total, width), BF16),
            sds((total, width), BF16),
            sds((total, width), F32),
            sds((n, width), BF16),
            sds((members * shape.tiles, QUAD * BLOCK), BF16),
        ],
        (where, ids),
        (*nf, *adj, prev, nxt, msg_weight, out_weight),
        [pltpu.VMEM((shape.ext, width), BF16), pltpu.VMEM((total + BLOCK, width), F32)],
        7 * unit,
        limit,
    )
    grad_pre, keep, give = call(
        functools.partial(upstream_kernel, shape, cot_layout),
        [sds((total, width), BF16), sds((half, width), F32), sds((half, width), F32)],
        (where,),
        (*cot, rowsum, hidden, slope, out_weight),
        [pltpu.VMEM((total, width), BF16)],
        2 * unit,
        limit,
    )
    pair = rounded(keep + swap(give, "region", 1))
    layers = [pair] + [swap(pair, "region", 2 * k) for k in range(1, regions // 2)]
    reduced = rounded(tree_sum([v.astype(F32) for v in layers]))
    across = swap(reduced, "region", 1)
    beside = swap(reduced, "grp", 1)
    diagonal = [
        (r * members + m, (r ^ 1) * members + (m ^ 1))
        for r in range(regions)
        for m in range(members)
    ]
    both = lax.ppermute(reduced, ("region", "grp"), diagonal)
    own, rim = call(
        functools.partial(backward_kernel, shape),
        [sds((n, width), F32), sds((h, width), BF16)],
        (where, ids),
        (tiles, grad_pre),
        [pltpu.VMEM((shape.ext + BLOCK, width), F32)],
        3 * unit,
        limit,
    )
    pairs = []
    for r in range(regions - 1):
        pairs.append((r * members + members - 1, (r + 1) * members))
        pairs.append(((r + 1) * members, r * members + members - 1))
    arrived = lax.ppermute(rim, ("region", "grp"), pairs)
    (grad_nodes,) = call(
        functools.partial(nodes_kernel, shape),
        [sds((n, width), BF16)],
        (where,),
        (own, arrived, cotangent, msg_weight),
        [],
        2 * unit,
        limit,
    )
    grad_msg_weight, grad_out_weight = call(
        weights_kernel,
        [sds((width, width), F32), sds((width, width), F32)],
        (where,),
        (reduced, across, beside, both),
        [],
        0,
        limit,
    )
    return (layer_out, grad_nodes, grad_msg_weight, grad_out_weight)


def solution(mesh):
    in_specs = (
        P(("region", "grp"), None),
        P(),
        P(),
        P(("region", "grp"), None),
        P(("region", "grp")),
        P(("region", "grp")),
        P(("region", "grp"), None),
        P(("region", "grp"), None),
    )
    out_specs = (P(("region", "grp"), None), P(("region", "grp"), None), P(), P())
    return jax.shard_map(
        per_device, mesh=mesh, in_specs=in_specs, out_specs=out_specs, check_vma=False
    )
```

```python
import functools

import jax
import jax.numpy as jnp
from jax import lax
from jax.experimental import pallas as pl
from jax.experimental.pallas import tpu as pltpu
from jax.sharding import PartitionSpec as P

BLOCK = 64
HALO_BLOCKS = 2
QUAD = 4
ID_ROWS = 16
BF16 = jnp.bfloat16
F32 = jnp.float32
VMEM = pl.BlockSpec(memory_space=pltpu.VMEM)
SMEM = pl.BlockSpec(memory_space=pltpu.SMEM)


def dot(a, b, ca=1, cb=0):
    return lax.dot_general(a, b, (((ca,), (cb,)), ((), ())), preferred_element_type=F32)


def aligned(value, unit):
    return value if isinstance(value, int) else pl.multiple_of(value, unit)


class Shape:
    def __init__(self, n, width, slots, members, regions):
        self.n, self.width, self.slots = n, width, slots
        self.members, self.regions = members, regions
        self.quads = slots // QUAD
        self.per_owner = slots // members
        self.halo = HALO_BLOCKS * BLOCK
        self.total = members * n
        self.ext = self.total + 2 * self.halo
        self.tiles = self.quads * BLOCK


def for_each_quad(shape, me, ids, tiles, body):
    lane = lax.broadcasted_iota(jnp.int32, (BLOCK, QUAD * BLOCK), 1) // BLOCK
    masks = [jnp.where(lane == j, 1.0, 0.0).astype(BF16) for j in range(QUAD)]

    def step(p, q):
        first = aligned((p * shape.quads + q) * BLOCK, BLOCK)
        tile = tiles[pl.ds(first, BLOCK), :]
        diagonal = jnp.concatenate([tile * m for m in masks], axis=0)
        place = p ^ me
        rows, cols, used = [], [], []
        for j in range(QUAD):
            slot = q * QUAD + j
            rows.append(pl.multiple_of(ids[place, slot] * BLOCK, BLOCK))
            cols.append(pl.multiple_of(ids[place, shape.slots + slot] * BLOCK, BLOCK))
            if isinstance(slot, int):
                owner, nth = divmod(slot, shape.per_owner)
            else:
                owner, nth = lax.div(slot, shape.per_owner), lax.rem(slot, shape.per_owner)
            used.append(nth < ids[place, 2 * shape.slots + owner])
        body(diagonal, rows, cols, used)

    if shape.members * shape.quads <= 32:
        for p in range(shape.members):
            for q in range(shape.quads):
                step(p, q)
    else:

        def flat(i, carry):
            step(lax.div(i, shape.quads), lax.rem(i, shape.quads))
            return carry

        lax.fori_loop(0, shape.members * shape.quads, flat, 0)


def put(me, layout, refs, into, size, first=0):
    for (k, start, rows), ref in zip(layout, refs):
        rows = min(rows, size - start)
        at = pl.multiple_of((me ^ k) * size + start + first, 8)
        into[pl.ds(at, rows), :] = ref[:rows, :]


def forward_kernel(shape, nf_layout, adj_layout, where, ids, *refs):
    nf, refs = refs[: len(nf_layout)], refs[len(nf_layout) :]
    adj, refs = refs[: len(adj_layout)], refs[len(adj_layout) :]
    prev, nxt, wm, wo, rowsum, hidden, slope, layer_out, tiles, source, acc = refs
    me = where[0]
    h, n, total = shape.halo, shape.n, shape.total
    source[:h, :] = prev[...]
    put(me, nf_layout, nf, source, n, h)
    source[h + total :, :] = nxt[...]
    put(me, adj_layout, adj, tiles, shape.tiles)
    acc[...] = jnp.zeros_like(acc)

    def add(diagonal, rows, cols, used):
        taken = jnp.concatenate([source[pl.ds(c, BLOCK), :] for c in cols], axis=0)
        out = dot(diagonal, taken)
        for j in range(QUAD):
            at = pl.ds(pl.multiple_of(jnp.where(used[j], rows[j], total), BLOCK), BLOCK)
            acc[at, :] += out[j * BLOCK : (j + 1) * BLOCK]

    for_each_quad(shape, me, ids, tiles, add)
    chunk = 256

    def finish(i, carry):
        at = pl.ds(pl.multiple_of(i * chunk, chunk), chunk)
        b = acc[at, :].astype(BF16)
        rowsum[at, :] = b
        agg = dot(b, wm[...])
        s = 0.5 * jnp.tanh(0.5 * agg) + 0.5
        hidden[at, :] = (agg * s).astype(BF16)
        slope[at, :] = s * (1.0 + agg * (1.0 - s))
        return carry

    lax.fori_loop(0, total // chunk, finish, 0, unroll=total // chunk <= 8)
    own = pl.ds(pl.multiple_of(me * n, n), n)
    layer_out[...] = (nf[0][...].astype(F32) + dot(hidden[own, :], wo[...])).astype(BF16)


def upstream_kernel(shape, layout, where, *refs):
    cot, refs = refs[: len(layout)], refs[len(layout) :]
    rowsum, hidden, slope, wo, grad_pre, keep, give, whole = refs
    me, core = where[0], where[1]
    put(me, layout, cot, whole, shape.n)
    chunk = min(shape.n, 512)
    for i in range(0, shape.total, chunk):
        up = dot(whole[i : i + chunk, :], wo[...], 1, 1)
        grad_pre[i : i + chunk, :] = (up * slope[i : i + chunk, :]).astype(BF16)
    half = shape.width // 2
    mine = pl.ds(pl.multiple_of(core * half, half), half)
    other = pl.ds(pl.multiple_of((1 - core) * half, half), half)

    @pl.when(me % 2 == 0)
    def _():
        give[...] = dot(rowsum[:, other], grad_pre[...], 0, 0)
        keep[...] = dot(rowsum[:, mine], grad_pre[...], 0, 0)

    @pl.when(me % 2 == 1)
    def _():
        give[...] = dot(hidden[:, other], whole[...], 0, 0)
        keep[...] = dot(hidden[:, mine], whole[...], 0, 0)


def backward_kernel(shape, where, ids, tiles, grad_pre, own, rim, acc):
    me = where[0]
    h, n = shape.halo, shape.n
    acc[...] = jnp.zeros_like(acc)

    def add(diagonal, rows, cols, used):
        taken = jnp.concatenate([grad_pre[pl.ds(r, BLOCK), :] for r in rows], axis=0)
        out = dot(diagonal, taken, 0, 0)
        for j in range(QUAD):
            at = pl.ds(pl.multiple_of(jnp.where(used[j], cols[j], shape.ext), BLOCK), BLOCK)
            acc[at, :] += out[j * BLOCK : (j + 1) * BLOCK]

    for_each_quad(shape, me, ids, tiles, add)
    own[...] = acc[pl.ds(pl.multiple_of(h + me * n, BLOCK), n), :]
    first = jnp.where(me == 0, 0, h + shape.total)
    rim[...] = acc[pl.ds(pl.multiple_of(first, h), h), :].astype(BF16)


def nodes_kernel(shape, where, own, arrived, cot, wm, out):
    me = where[0]
    rim = arrived[...].astype(F32)
    head = jnp.where(me == 0, rim, 0.0)
    tail = jnp.where(me == shape.members - 1, rim, 0.0)
    zeros = jnp.zeros((shape.n - 2 * shape.halo, shape.width), F32)
    grad_msg = (own[...] + jnp.concatenate([head, zeros, tail], axis=0)).astype(BF16)
    out[...] = (cot[...].astype(F32) + dot(grad_msg, wm[...], 1, 1)).astype(BF16)


def weights_kernel(where, own, across, beside, both, msg, out):
    me, core = where[0], where[1]
    half = own.shape[0]
    mine = pl.ds(pl.multiple_of(core * half, half), half)
    other = pl.ds(pl.multiple_of((1 - core) * half, half), half)

    @pl.when(me % 2 == 0)
    def _():
        msg[mine, :] = own[...].astype(F32)
        msg[other, :] = across[...].astype(F32)
        out[mine, :] = beside[...].astype(F32)
        out[other, :] = both[...].astype(F32)

    @pl.when(me % 2 == 1)
    def _():
        out[mine, :] = own[...].astype(F32)
        out[other, :] = across[...].astype(F32)
        msg[mine, :] = beside[...].astype(F32)
        msg[other, :] = both[...].astype(F32)


def call(kernel, outs, scalars, args, scratch, flops, limit):
    moved = sum(a.size * a.dtype.itemsize for a in (*args, *outs))
    return pl.pallas_call(
        kernel,
        out_shape=outs,
        in_specs=[SMEM] * len(scalars) + [VMEM] * len(args),
        out_specs=[VMEM] * len(outs),
        scratch_shapes=scratch,
        compiler_params=pltpu.CompilerParams(vmem_limit_bytes=limit),
        cost_estimate=pl.CostEstimate(flops=flops, bytes_accessed=moved, transcendentals=0),
    )(*scalars, *args)


def swap(value, axis, k):
    return lax.ppermute(value, axis, [(i, i ^ k) for i in range(lax.axis_size(axis))])


def gather(value, after=()):
    members = lax.axis_size("grp")
    rows = value.shape[0]
    if members != 4:
        pieces = [value] + [swap(value, "grp", k) for k in range(1, members)]
        return pieces, tuple((k, 0, rows) for k in range(members))
    half = rows // 2
    x, y = swap(value, "grp", 1), swap(value, "grp", 2)
    low, high, _ = lax.optimization_barrier((x[:half], y[half:], after))
    low, high = swap(low, "grp", 2), swap(high, "grp", 1)
    layout = ((0, 0, rows), (1, 0, rows), (2, 0, rows), (3, 0, half), (3, half, rows - half))
    return [value, x, y, low, high], layout


def tree_sum(values):
    while len(values) > 1:
        values = [values[i] + values[i + 1] for i in range(0, len(values), 2)]
    return values[0]


def rounded(value):
    return lax.reduce_precision(value, 8, 7).astype(BF16)


def per_device(
    node_feats, msg_weight, out_weight, adj_blocks, block_row, block_col, live_counts, cotangent
):
    n, width = node_feats.shape
    slots = adj_blocks.shape[0]
    members, regions = lax.axis_size("grp"), lax.axis_size("region")
    shape = Shape(n, width, slots, members, regions)
    h, total = shape.halo, shape.total
    me, region = lax.axis_index("grp"), lax.axis_index("region")
    where = jnp.stack([me, region % 2]).astype(jnp.int32)
    limit = (20 << 20) if members <= 4 else (60 << 20)

    nf, nf_layout = gather(node_feats)

    tiles = adj_blocks.reshape(shape.quads, QUAD, BLOCK, BLOCK).transpose(0, 2, 1, 3)
    tiles = tiles.reshape(shape.tiles, QUAD * BLOCK)
    lanes = QUAD * BLOCK
    ids = jnp.concatenate([block_row, block_col, live_counts[0]])
    ids = lax.optimization_barrier(ids).astype(BF16)[None]
    ids = jnp.pad(ids, ((0, ID_ROWS - 1), (0, lanes - ids.shape[1])))
    adj, adj_layout = gather(jnp.concatenate([tiles, ids], axis=0))

    firsts, lasts = {}, {}
    for (k, start, rows), piece in zip(nf_layout, nf):
        if start == 0:
            firsts[k] = piece[:h]
        if start + rows == n:
            lasts[k] = piece[rows - h :]
    first, last = firsts[0], lasts[0]
    for k in range(1, members):
        first = jnp.where(me == k, firsts[k], first)
        last = jnp.where(me ^ k == members - 1, lasts[k], last)
    late = lax.optimization_barrier((cotangent, nf[3:]))[0]
    cot, cot_layout = gather(late)

    prev = lax.ppermute(last, "region", [(i, i + 1) for i in range(regions - 1)])
    nxt = lax.ppermute(first, "region", [(i + 1, i) for i in range(regions - 1)])

    held = adj[:3] + lax.optimization_barrier((adj[3:], nxt))[0]
    found = [
        a[shape.tiles - start : shape.tiles - start + 1]
        for (_, start, rows), a in zip(adj_layout, held)
        if start + rows > shape.tiles
    ]
    ids = jnp.concatenate(found, axis=0).astype(jnp.int32)

    sds = jax.ShapeDtypeStruct
    half = width // 2
    unit = members * shape.quads * 2 * 256**3
    rowsum, hidden, slope, layer_out, tiles = call(
        functools.partial(forward_kernel, shape, nf_layout, adj_layout),
        [
            sds((total, width), BF16),
            sds((total, width), BF16),
            sds((total, width), F32),
            sds((n, width), BF16),
            sds((members * shape.tiles, QUAD * BLOCK), BF16),
        ],
        (where, ids),
        (*nf, *adj, prev, nxt, msg_weight, out_weight),
        [pltpu.VMEM((shape.ext, width), BF16), pltpu.VMEM((total + BLOCK, width), F32)],
        7 * unit,
        limit,
    )
    grad_pre, keep, give = call(
        functools.partial(upstream_kernel, shape, cot_layout),
        [sds((total, width), BF16), sds((half, width), F32), sds((half, width), F32)],
        (where,),
        (*cot, rowsum, hidden, slope, out_weight),
        [pltpu.VMEM((total, width), BF16)],
        2 * unit,
        limit,
    )
    pair = rounded(keep + swap(give, "region", 1))
    layers = [pair] + [swap(pair, "region", 2 * k) for k in range(1, regions // 2)]
    reduced = rounded(tree_sum([v.astype(F32) for v in layers]))
    across = swap(reduced, "region", 1)
    beside = swap(reduced, "grp", 1)
    diagonal = [
        (r * members + m, (r ^ 1) * members + (m ^ 1))
        for r in range(regions)
        for m in range(members)
    ]
    both = lax.ppermute(reduced, ("region", "grp"), diagonal)
    own, rim = call(
        functools.partial(backward_kernel, shape),
        [sds((n, width), F32), sds((h, width), BF16)],
        (where, ids),
        (tiles, grad_pre),
        [pltpu.VMEM((shape.ext + BLOCK, width), F32)],
        3 * unit,
        limit,
    )
    pairs = []
    for r in range(regions - 1):
        pairs.append((r * members + members - 1, (r + 1) * members))
        pairs.append(((r + 1) * members, r * members + members - 1))
    arrived = lax.ppermute(rim, ("region", "grp"), pairs)
    (grad_nodes,) = call(
        functools.partial(nodes_kernel, shape),
        [sds((n, width), BF16)],
        (where,),
        (own, arrived, cotangent, msg_weight),
        [],
        2 * unit,
        limit,
    )
    grad_msg_weight, grad_out_weight = call(
        weights_kernel,
        [sds((width, width), F32), sds((width, width), F32)],
        (where,),
        (reduced, across, beside, both),
        [],
        0,
        limit,
    )
    return (layer_out, grad_nodes, grad_msg_weight, grad_out_weight)


def solution(mesh):
    in_specs = (
        P(("region", "grp"), None),
        P(),
        P(),
        P(("region", "grp"), None),
        P(("region", "grp")),
        P(("region", "grp")),
        P(("region", "grp"), None),
        P(("region", "grp"), None),
    )
    out_specs = (P(("region", "grp"), None), P(("region", "grp"), None), P(), P())
    return jax.shard_map(
        per_device, mesh=mesh, in_specs=in_specs, out_specs=out_specs, check_vma=False
    )
```

```python
import functools

import jax
import jax.numpy as jnp
from jax import lax
from jax.experimental import pallas as pl
from jax.experimental.pallas import tpu as pltpu
from jax.sharding import PartitionSpec as P

BLOCK = 64
HALO_BLOCKS = 2
QUAD = 4
ID_ROWS = 16
BF16 = jnp.bfloat16
F32 = jnp.float32
VMEM = pl.BlockSpec(memory_space=pltpu.VMEM)
SMEM = pl.BlockSpec(memory_space=pltpu.SMEM)


def dot(a, b, ca=1, cb=0):
    return lax.dot_general(a, b, (((ca,), (cb,)), ((), ())), preferred_element_type=F32)


def aligned(value, unit):
    return value if isinstance(value, int) else pl.multiple_of(value, unit)


class Shape:
    def __init__(self, n, width, slots, members, regions):
        self.n, self.width, self.slots = n, width, slots
        self.members, self.regions = members, regions
        self.quads = slots // QUAD
        self.per_owner = slots // members
        self.halo = HALO_BLOCKS * BLOCK
        self.total = members * n
        self.ext = self.total + 2 * self.halo
        self.tiles = self.quads * BLOCK


def for_each_quad(shape, me, ids, tiles, body):
    lane = lax.broadcasted_iota(jnp.int32, (BLOCK, QUAD * BLOCK), 1) // BLOCK
    masks = [jnp.where(lane == j, 1.0, 0.0).astype(BF16) for j in range(QUAD)]

    def step(p, q):
        first = aligned((p * shape.quads + q) * BLOCK, BLOCK)
        tile = tiles[pl.ds(first, BLOCK), :]
        diagonal = jnp.concatenate([tile * m for m in masks], axis=0)
        place = p ^ me
        rows, cols, used = [], [], []
        for j in range(QUAD):
            slot = q * QUAD + j
            rows.append(pl.multiple_of(ids[place, slot] * BLOCK, BLOCK))
            cols.append(pl.multiple_of(ids[place, shape.slots + slot] * BLOCK, BLOCK))
            if isinstance(slot, int):
                owner, nth = divmod(slot, shape.per_owner)
            else:
                owner, nth = lax.div(slot, shape.per_owner), lax.rem(slot, shape.per_owner)
            used.append(nth < ids[place, 2 * shape.slots + owner])
        body(diagonal, rows, cols, used)

    if shape.members * shape.quads <= 32:
        for p in range(shape.members):
            for q in range(shape.quads):
                step(p, q)
    else:

        def flat(i, carry):
            step(lax.div(i, shape.quads), lax.rem(i, shape.quads))
            return carry

        lax.fori_loop(0, shape.members * shape.quads, flat, 0)


def put(me, layout, refs, into, size, first=0):
    for (k, start, rows), ref in zip(layout, refs):
        rows = min(rows, size - start)
        at = pl.multiple_of((me ^ k) * size + start + first, 8)
        into[pl.ds(at, rows), :] = ref[:rows, :]


def forward_kernel(shape, nf_layout, adj_layout, where, ids, *refs):
    nf, refs = refs[: len(nf_layout)], refs[len(nf_layout) :]
    adj, refs = refs[: len(adj_layout)], refs[len(adj_layout) :]
    prev, nxt, wm, wo, rowsum, hidden, slope, layer_out, tiles, source, acc = refs
    me = where[0]
    h, n, total = shape.halo, shape.n, shape.total
    source[:h, :] = prev[...]
    put(me, nf_layout, nf, source, n, h)
    source[h + total :, :] = nxt[...]
    put(me, adj_layout, adj, tiles, shape.tiles)
    acc[...] = jnp.zeros_like(acc)

    def add(diagonal, rows, cols, used):
        taken = jnp.concatenate([source[pl.ds(c, BLOCK), :] for c in cols], axis=0)
        out = dot(diagonal, taken)
        for j in range(QUAD):
            at = pl.ds(pl.multiple_of(jnp.where(used[j], rows[j], total), BLOCK), BLOCK)
            acc[at, :] += out[j * BLOCK : (j + 1) * BLOCK]

    for_each_quad(shape, me, ids, tiles, add)
    chunk = 256

    def finish(i, carry):
        at = pl.ds(pl.multiple_of(i * chunk, chunk), chunk)
        b = acc[at, :].astype(BF16)
        rowsum[at, :] = b
        agg = dot(b, wm[...])
        s = 0.5 * jnp.tanh(0.5 * agg) + 0.5
        hidden[at, :] = (agg * s).astype(BF16)
        slope[at, :] = s * (1.0 + agg * (1.0 - s))
        return carry

    lax.fori_loop(0, total // chunk, finish, 0, unroll=total // chunk <= 8)
    own = pl.ds(pl.multiple_of(me * n, n), n)
    layer_out[...] = (nf[0][...].astype(F32) + dot(hidden[own, :], wo[...])).astype(BF16)


def upstream_kernel(shape, layout, where, *refs):
    cot, refs = refs[: len(layout)], refs[len(layout) :]
    rowsum, hidden, slope, wo, grad_pre, keep, give, whole = refs
    me, core = where[0], where[1]
    put(me, layout, cot, whole, shape.n)
    chunk = min(shape.n, 512)
    for i in range(0, shape.total, chunk):
        up = dot(whole[i : i + chunk, :], wo[...], 1, 1)
        grad_pre[i : i + chunk, :] = (up * slope[i : i + chunk, :]).astype(BF16)
    half = shape.width // 2
    mine = pl.ds(pl.multiple_of(core * half, half), half)
    other = pl.ds(pl.multiple_of((1 - core) * half, half), half)

    @pl.when(me % 2 == 0)
    def _():
        give[...] = dot(rowsum[:, other], grad_pre[...], 0, 0)
        keep[...] = dot(rowsum[:, mine], grad_pre[...], 0, 0)

    @pl.when(me % 2 == 1)
    def _():
        give[...] = dot(hidden[:, other], whole[...], 0, 0)
        keep[...] = dot(hidden[:, mine], whole[...], 0, 0)


def backward_kernel(shape, where, ids, tiles, grad_pre, own, rim, acc):
    me = where[0]
    h, n = shape.halo, shape.n
    acc[...] = jnp.zeros_like(acc)

    def add(diagonal, rows, cols, used):
        taken = jnp.concatenate([grad_pre[pl.ds(r, BLOCK), :] for r in rows], axis=0)
        out = dot(diagonal, taken, 0, 0)
        for j in range(QUAD):
            at = pl.ds(pl.multiple_of(jnp.where(used[j], cols[j], shape.ext), BLOCK), BLOCK)
            acc[at, :] += out[j * BLOCK : (j + 1) * BLOCK]

    for_each_quad(shape, me, ids, tiles, add)
    own[...] = acc[pl.ds(pl.multiple_of(h + me * n, BLOCK), n), :]
    first = jnp.where(me == 0, 0, h + shape.total)
    rim[...] = acc[pl.ds(pl.multiple_of(first, h), h), :].astype(BF16)


def nodes_kernel(shape, where, own, arrived, cot, wm, out):
    me = where[0]
    rim = arrived[...].astype(F32)
    head = jnp.where(me == 0, rim, 0.0)
    tail = jnp.where(me == shape.members - 1, rim, 0.0)
    zeros = jnp.zeros((shape.n - 2 * shape.halo, shape.width), F32)
    grad_msg = (own[...] + jnp.concatenate([head, zeros, tail], axis=0)).astype(BF16)
    out[...] = (cot[...].astype(F32) + dot(grad_msg, wm[...], 1, 1)).astype(BF16)


def weights_kernel(where, own, across, beside, both, msg, out):
    me, core = where[0], where[1]
    half = own.shape[0]
    mine = pl.ds(pl.multiple_of(core * half, half), half)
    other = pl.ds(pl.multiple_of((1 - core) * half, half), half)

    @pl.when(me % 2 == 0)
    def _():
        msg[mine, :] = own[...].astype(F32)
        msg[other, :] = across[...].astype(F32)
        out[mine, :] = beside[...].astype(F32)
        out[other, :] = both[...].astype(F32)

    @pl.when(me % 2 == 1)
    def _():
        out[mine, :] = own[...].astype(F32)
        out[other, :] = across[...].astype(F32)
        msg[mine, :] = beside[...].astype(F32)
        msg[other, :] = both[...].astype(F32)


def call(kernel, outs, scalars, args, scratch, flops, limit):
    moved = sum(a.size * a.dtype.itemsize for a in (*args, *outs))
    return pl.pallas_call(
        kernel,
        out_shape=outs,
        in_specs=[SMEM] * len(scalars) + [VMEM] * len(args),
        out_specs=[VMEM] * len(outs),
        scratch_shapes=scratch,
        compiler_params=pltpu.CompilerParams(vmem_limit_bytes=limit),
        cost_estimate=pl.CostEstimate(flops=flops, bytes_accessed=moved, transcendentals=0),
    )(*scalars, *args)


def swap(value, axis, k):
    return lax.ppermute(value, axis, [(i, i ^ k) for i in range(lax.axis_size(axis))])


def gather(value, after=()):
    members = lax.axis_size("grp")
    rows = value.shape[0]
    if members != 4:
        pieces = [value] + [swap(value, "grp", k) for k in range(1, members)]
        return pieces, tuple((k, 0, rows) for k in range(members))
    half = rows // 2
    x, y = swap(value, "grp", 1), swap(value, "grp", 2)
    low, high, _ = lax.optimization_barrier((x[:half], y[half:], after))
    low, high = swap(low, "grp", 2), swap(high, "grp", 1)
    layout = ((0, 0, rows), (1, 0, rows), (2, 0, rows), (3, 0, half), (3, half, rows - half))
    return [value, x, y, low, high], layout


def tree_sum(values):
    while len(values) > 1:
        values = [values[i] + values[i + 1] for i in range(0, len(values), 2)]
    return values[0]


def rounded(value):
    return lax.reduce_precision(value, 8, 7).astype(BF16)


def per_device(
    node_feats, msg_weight, out_weight, adj_blocks, block_row, block_col, live_counts, cotangent
):
    n, width = node_feats.shape
    slots = adj_blocks.shape[0]
    members, regions = lax.axis_size("grp"), lax.axis_size("region")
    shape = Shape(n, width, slots, members, regions)
    h, total = shape.halo, shape.total
    me, region = lax.axis_index("grp"), lax.axis_index("region")
    where = jnp.stack([me, region % 2]).astype(jnp.int32)
    limit = (20 << 20) if members <= 4 else (60 << 20)

    nf, nf_layout = gather(node_feats)

    tiles = adj_blocks.reshape(shape.quads, QUAD, BLOCK, BLOCK).transpose(0, 2, 1, 3)
    tiles = tiles.reshape(shape.tiles, QUAD * BLOCK)
    lanes = QUAD * BLOCK
    ids = jnp.concatenate([block_row, block_col, live_counts[0]])
    ids = lax.optimization_barrier(ids).astype(BF16)[None]
    ids = jnp.pad(ids, ((0, ID_ROWS - 1), (0, lanes - ids.shape[1])))
    adj, adj_layout = gather(jnp.concatenate([tiles, ids], axis=0))

    firsts, lasts = {}, {}
    for (k, start, rows), piece in zip(nf_layout, nf):
        if start == 0:
            firsts[k] = piece[:h]
        if start + rows == n:
            lasts[k] = piece[rows - h :]
    first, last = firsts[0], lasts[0]
    for k in range(1, members):
        first = jnp.where(me == k, firsts[k], first)
        last = jnp.where(me ^ k == members - 1, lasts[k], last)
    late = lax.optimization_barrier((cotangent, nf[3:]))[0]
    cot, cot_layout = gather(late)

    prev = lax.ppermute(last, "region", [(i, i + 1) for i in range(regions - 1)])
    nxt = lax.ppermute(first, "region", [(i + 1, i) for i in range(regions - 1)])

    held = adj[:3] + lax.optimization_barrier((adj[3:], cot[1], nxt))[0]
    found = [
        a[shape.tiles - start : shape.tiles - start + 1]
        for (_, start, rows), a in zip(adj_layout, held)
        if start + rows > shape.tiles
    ]
    ids = jnp.concatenate(found, axis=0).astype(jnp.int32)

    sds = jax.ShapeDtypeStruct
    half = width // 2
    unit = members * shape.quads * 2 * 256**3
    rowsum, hidden, slope, layer_out, tiles = call(
        functools.partial(forward_kernel, shape, nf_layout, adj_layout),
        [
            sds((total, width), BF16),
            sds((total, width), BF16),
            sds((total, width), F32),
            sds((n, width), BF16),
            sds((members * shape.tiles, QUAD * BLOCK), BF16),
        ],
        (where, ids),
        (*nf, *adj, prev, nxt, msg_weight, out_weight),
        [pltpu.VMEM((shape.ext, width), BF16), pltpu.VMEM((total + BLOCK, width), F32)],
        7 * unit,
        limit,
    )
    grad_pre, keep, give = call(
        functools.partial(upstream_kernel, shape, cot_layout),
        [sds((total, width), BF16), sds((half, width), F32), sds((half, width), F32)],
        (where,),
        (*cot, rowsum, hidden, slope, out_weight),
        [pltpu.VMEM((total, width), BF16)],
        2 * unit,
        limit,
    )
    pair = rounded(keep + swap(give, "region", 1))
    layers = [pair] + [swap(pair, "region", 2 * k) for k in range(1, regions // 2)]
    reduced = rounded(tree_sum([v.astype(F32) for v in layers]))
    across = swap(reduced, "region", 1)
    beside = swap(reduced, "grp", 1)
    diagonal = [
        (r * members + m, (r ^ 1) * members + (m ^ 1))
        for r in range(regions)
        for m in range(members)
    ]
    both = lax.ppermute(reduced, ("region", "grp"), diagonal)
    own, rim = call(
        functools.partial(backward_kernel, shape),
        [sds((n, width), F32), sds((h, width), BF16)],
        (where, ids),
        (tiles, grad_pre),
        [pltpu.VMEM((shape.ext + BLOCK, width), F32)],
        3 * unit,
        limit,
    )
    pairs = []
    for r in range(regions - 1):
        pairs.append((r * members + members - 1, (r + 1) * members))
        pairs.append(((r + 1) * members, r * members + members - 1))
    arrived = lax.ppermute(rim, ("region", "grp"), pairs)
    (grad_nodes,) = call(
        functools.partial(nodes_kernel, shape),
        [sds((n, width), BF16)],
        (where,),
        (own, arrived, cotangent, msg_weight),
        [],
        2 * unit,
        limit,
    )
    grad_msg_weight, grad_out_weight = call(
        weights_kernel,
        [sds((width, width), F32), sds((width, width), F32)],
        (where,),
        (reduced, across, beside, both),
        [],
        0,
        limit,
    )
    return (layer_out, grad_nodes, grad_msg_weight, grad_out_weight)


def solution(mesh):
    in_specs = (
        P(("region", "grp"), None),
        P(),
        P(),
        P(("region", "grp"), None),
        P(("region", "grp")),
        P(("region", "grp")),
        P(("region", "grp"), None),
        P(("region", "grp"), None),
    )
    out_specs = (P(("region", "grp"), None), P(("region", "grp"), None), P(), P())
    return jax.shard_map(
        per_device, mesh=mesh, in_specs=in_specs, out_specs=out_specs, check_vma=False
    )
```
